32 devices in a mesh: pb: 8 (over y, x, core), kv: 4 (over z).
Axes of the slice: x: 2, y: 2, z: 4, core: 2. Of those that a mesh axis runs over, the one named last changes fastest.
Arguments:
- queries: bfloat16 [4096, 1024], P(('pb', 'kv')), may hold values from -6 to 6
- key_rows: bfloat16 [4096, 128], P(('kv', 'pb')), may hold values from -6 to 6
- value_rows: bfloat16 [4096, 128], P(('kv', 'pb')), may hold values from -0.59765625 to 0.59765625
- output: bfloat16 [4096, 1024], P(('pb', 'kv')), may hold values from -1.796875 to 1.796875
- out_grad: bfloat16 [4096, 1024], P(('pb', 'kv')), may hold values from -6 to 6
- log_norm: float32 [8, 4096], P(None, ('pb', 'kv')), as said below
- positions: int32 [4096], replicated, may hold values from 0 to 4095, as said below
Outputs:
- query_grad: float32 [4096, 1024], P(('pb', 'kv'))
- key_grad: float32 [4096, 128], P(('kv', 'pb'))
- value_grad: float32 [4096, 128], P(('kv', 'pb'))
The draws below stay inside these ranges and needn't reach their ends.
Inputs may be any that keep to these rules, and one draw needn't show every extreme that they name: A permutation of 0 to 4095: row r holds the token at position positions[r]. log_norm[h, r] - log(1 + positions[r]) lies between 0.25 and 0.75.
All inputs are finite; a program needn't handle non-finite values.
Results may differ from the reference program's by a relative error of at most 0.0041.
Values may be sent and summed in bfloat16 or wider, within the bound.
A program may use at most 64 MiB of HBM per device.

```python
import math
import jax
import jax.numpy as jnp
from jax import lax

HD = 128
GROUP = 8
S = 4096
QTOK = 512
N_PB = 8


def shared_order(key):
    return jax.random.permutation(jax.random.fold_in(key, 7), S).astype(jnp.int32)


def draw_positions(key, part):
    return shared_order(key)


def draw_log_norm(key, part):
    token_pos = shared_order(key).astype(jnp.float32)
    offset_key = jax.random.fold_in(key, 9)
    offsets = jax.random.uniform(offset_key, (GROUP, S), jnp.float32, 0.25, 0.75)
    return jnp.log(token_pos + 1.0)[None, :] + offsets


def level_of(rng, dims, pieces, low, largest):
    level, own = 1.0, jax.random.fold_in(rng, 6)
    for position, parts in pieces:
        steps = jnp.exp(jax.random.uniform(jax.random.fold_in(own, position), (parts,), jnp.float32, low / len(pieces), largest / len(pieces)))
        level = level * jnp.repeat(steps, dims[position] // parts).reshape([-1 if axis == position else 1 for axis in range(len(dims))])
    return level


def noise(key, dims, spread, bound, shards=(), held_as=jnp.bfloat16):
    entries = jax.random.normal(key, dims, jnp.float32) * spread
    if len(shards) > 0:
        entries = level_of(key, dims, shards, -0.22, 0.18) * entries
    return jnp.clip(entries, min=-bound, max=bound).astype(held_as)


def setup_inputs(seed: int = 0) -> dict:
    key_list = jax.random.split(jax.random.key(seed), 8)
    return {
        "queries": noise(key_list[0], (S, GROUP * HD), 1.0, 6.0, ((0, 32),)),
        "key_rows": noise(key_list[1], (S, HD), 1.0, 6.0, ((0, 32),)),
        "value_rows": noise(key_list[2], (S, HD), 0.1, 0.59765625, ((0, 32),)),
        "output": noise(key_list[3], (S, GROUP * HD), 0.3, 1.796875, ((0, 32),)),
        "out_grad": noise(key_list[4], (S, GROUP * HD), 1.0, 6.0, ((0, 32),)),
        "log_norm": draw_log_norm(jax.random.fold_in(key_list[7], 71), 0),
        "positions": draw_positions(jax.random.fold_in(key_list[7], 71), 0),
    }


def reference(queries, key_rows, value_rows, output, out_grad, log_norm, positions):
    inv_root = 1.0 / math.sqrt(HD)
    rows_block = math.gcd(QTOK, 256)
    inner_blocks = QTOK // rows_block
    query_all = queries.astype(jnp.float32).reshape(N_PB, inner_blocks, rows_block, GROUP, HD)
    grad_all = out_grad.astype(jnp.float32).reshape(N_PB, inner_blocks, rows_block, GROUP, HD)
    saved_all = output.astype(jnp.float32).reshape(N_PB, inner_blocks, rows_block, GROUP, HD)
    key_all = key_rows.astype(jnp.float32)
    value_all = value_rows.astype(jnp.float32)
    row_delta = lax.optimization_barrier(jnp.sum(grad_all * saved_all, axis=4))
    norm_blocks = log_norm.T.reshape(N_PB, inner_blocks, rows_block, GROUP)
    pos_blocks = positions.reshape(N_PB, inner_blocks, rows_block)

    def one_block(running, inputs):
        key_sum, value_sum = running
        query_block, grad_block, delta_block, norm_block, pos_block = inputs
        scores = jnp.einsum('tgd,cd->tgc', query_block, key_all) * inv_root
        visible = (positions[None, :] <= pos_block[:, None])[:, None, :]
        probs_full = jnp.where(visible, jnp.exp(scores - norm_block[:, :, None]), jnp.float32(0.0))
        probs_low = lax.optimization_barrier(probs_full.astype(jnp.bfloat16)).astype(jnp.float32)
        value_sum = value_sum + jnp.einsum('tgc,tgd->cd', probs_low, grad_block)
        grad_probs = jnp.einsum('tgd,cd->tgc', grad_block, value_all)
        grad_scores = probs_full * (grad_probs - delta_block[:, :, None]) * inv_root
        grad_scores = lax.optimization_barrier(grad_scores.astype(jnp.bfloat16)).astype(jnp.float32)
        query_part = jnp.einsum('tgc,cd->tgd', grad_scores, key_all).reshape(rows_block, GROUP * HD)
        key_sum = key_sum + jnp.einsum('tgc,tgd->cd', grad_scores, query_block)
        return ((key_sum, value_sum), query_part)
    empty_grad = jnp.zeros((S, HD), jnp.float32)

    def one_stripe(totals, inputs):
        key_total, value_total = totals
        (key_sum, value_sum), query_parts = lax.scan(one_block, (empty_grad, empty_grad), inputs)
        return ((key_total + key_sum, value_total + value_sum), query_parts)
    (key_total, value_total), query_parts = lax.scan(one_stripe, (empty_grad, empty_grad), (query_all, grad_all, row_delta, norm_blocks, pos_blocks))
    return (query_parts.reshape(S, GROUP * HD), key_total, value_total)
```

```python
import functools
import math

import jax
import jax.numpy as jnp
from jax import lax
from jax.experimental import pallas as pl
from jax.experimental.pallas import tpu as pltpu
from jax.sharding import PartitionSpec as P

MESH = pl.DeviceIdType.MESH
LOG2E = math.log2(math.e)
HIDDEN = -1e30


def flip(index, mask, count):
    total, bit = 0, 1
    while bit < count:
        digit = (index // bit) % 2
        total = total + bit * ((1 - digit) if mask & bit else digit)
        bit *= 2
    return total


def kernel(
    planes, layers, q_ref, k_ref, v_ref, o_ref, g_ref, n_ref, pos_ref,
    dq_ref, dk_ref, dv_ref,
    q_all, g_all, k_all, v_all, norm, delta, bias, dk_acc, dv_acc, dq_acc, dq_in,
    own, out1, in1, out2, in2,
    pair_send, pair_recv, z_send, z_recv, p_send, p_recv, r1_send, r1_recv, r2_send, r2_recv,
):
    pb, z = lax.axis_index("pb"), lax.axis_index("kv")
    p, core = pb // 2, pb % 2
    rows, heads = q_ref.shape[0], n_ref.shape[0]
    keys, width = k_ref.shape
    inv_root = 1.0 / math.sqrt(width)

    partner = {"pb": p * 2 + 1 - core, "kv": z}
    z_peers = [(z + step) % layers for step in range(layers)]
    p_peers = [flip(p, step, planes) for step in range(planes)]

    def above(step):
        return {"pb": pb, "kv": z_peers[step]}

    def beside(step):
        return {"pb": p_peers[step] * 2 + core, "kv": z}

    def remote(src, dst, send, recv, device):
        return pltpu.make_async_remote_copy(
            src_ref=src, dst_ref=dst, send_sem=send, recv_sem=recv,
            device_id=device, device_id_type=MESH,
        )

    peers = [partner] + [above(s) for s in range(1, layers)] + [beside(s) for s in range(1, planes)]
    barrier = pltpu.get_barrier_semaphore()
    for peer in peers:
        pl.semaphore_signal(barrier, inc=1, device_id=peer, device_id_type=MESH)
    pl.semaphore_wait(barrier, len(peers))

    def key_rows_of(layer):
        return pl.ds(pl.multiple_of(layer * keys, keys), keys)

    pending = []
    mine = key_rows_of(z)
    z_copies = {}
    for step in range(1, layers):
        pair = [
            remote(src, dst.at[p, mine], z_send.at[step - 1, i], z_recv.at[step - 1, i], above(step))
            for i, (src, dst) in enumerate(((k_ref, k_all), (v_ref, v_all)))
        ]
        for copy in pair:
            copy.start()
        z_copies[step] = pair
    p_copies = {}

    def spread(step_z):
        layer = (z + layers - step_z) % layers
        place = key_rows_of(layer)
        for step in range(1, planes):
            pair = []
            for i, (own, full) in enumerate(((k_ref, k_all), (v_ref, v_all))):
                src = own if step_z == 0 else full.at[p, place]
                copy = remote(
                    src, full.at[p, place], p_send.at[step - 1, step_z, i],
                    p_recv.at[step - 1, step_z, i], beside(step),
                )
                copy.start()
                pair.append(copy)
            p_copies[step, step_z] = pair

    spread(0)
    pair_copies = [
        remote(q_ref, q_all.at[pl.ds(rows, rows)], pair_send.at[0], pair_recv.at[0], partner),
        remote(g_ref, g_all.at[pl.ds(rows, rows)], pair_send.at[1], pair_recv.at[1], partner),
    ]
    for copy in pair_copies:
        copy.start()

    norm[:, :rows] = n_ref[...] * LOG2E
    for h in range(heads):
        part = slice(h * width, (h + 1) * width)
        product = g_ref[:, part].astype(jnp.float32) * o_ref[:, part].astype(jnp.float32)
        delta[h : h + 1, :rows] = jnp.sum(product.T, axis=0, keepdims=True)
    stat_copies = [
        remote(norm.at[:, pl.ds(0, rows)], norm.at[:, pl.ds(rows, rows)], pair_send.at[2], pair_recv.at[2], partner),
        remote(delta.at[:, pl.ds(0, rows)], delta.at[:, pl.ds(rows, rows)], pair_send.at[3], pair_recv.at[3], partner),
    ]
    for copy in stat_copies:
        copy.start()
    pair_copies += stat_copies
    q_all[:rows] = q_ref[...]
    g_all[:rows] = g_ref[...]
    k_all[p, mine] = k_ref[...]
    v_all[p, mine] = v_ref[...]

    pos_own = pos_ref[pl.ds(pb * layers + z, 1), :]
    pos_partner = pos_ref[pl.ds((p * 2 + 1 - core) * layers + z, 1), :]

    def make_bias(column):
        for layer in range(layers):
            block = layer * (2 * planes) + column * 2 + core
            row = pos_ref[pl.ds(block, 1), :]
            key_pos = jnp.broadcast_to(row, (rows, keys)).T
            place = slice(layer * keys, (layer + 1) * keys)
            bias[place, :rows] = jnp.where(key_pos <= pos_own, 0.0, HIDDEN)
            bias[place, rows:] = jnp.where(key_pos <= pos_partner, 0.0, HIDDEN)

    make_bias(p)
    for step in range(1, layers):
        for copy in z_copies[step]:
            copy.wait_recv()
        spread(step)
    for copy in pair_copies:
        copy.wait_recv()

    last = (((1,), (1,)), ((), ()))

    def compute(column, first):
        k_turned = k_all[column].T

        def one_head(h):
            part = pl.ds(pl.multiple_of(h * width, width), width)
            q, g = q_all[:, part], g_all[:, part]
            scores = lax.dot_general(k_all[column], q, last, preferred_element_type=jnp.float32)
            grad_probs = lax.dot_general(v_all[column], g, last, preferred_element_type=jnp.float32)
            probs = jnp.exp2(scores * (inv_root * LOG2E) - norm[pl.ds(h, 1), :] + bias[...])
            probs_low = probs.astype(jnp.bfloat16)
            grad_scores = (probs * (grad_probs - delta[pl.ds(h, 1), :])).astype(jnp.bfloat16)
            dv = jnp.dot(probs_low, g, preferred_element_type=jnp.float32)
            dk = jnp.dot(grad_scores, q, preferred_element_type=jnp.float32)
            dq = jnp.dot(k_turned, grad_scores, preferred_element_type=jnp.float32)
            return dv, dk, dq

        dk_acc[...] = jnp.zeros_like(dk_acc)
        dv_acc[...] = jnp.zeros_like(dv_acc)

        def body(i, carry):
            results = [one_head(2 * i), one_head(2 * i + 1)]
            dv_acc[...] += results[0][0] + results[1][0]
            dk_acc[...] += results[0][1] + results[1][1]
            for j in range(2):
                dq = results[j][2]
                for side in range(2):
                    half = dq[:, side * rows : (side + 1) * rows]
                    if first:
                        dq_acc[side, 2 * i + j] = half
                    else:
                        dq_acc[side, 2 * i + j] += half
            return carry

        lax.fori_loop(0, heads // 2, body, 0)

    compute(p, True)
    own[0] = dk_acc[...]
    own[1] = dv_acc[...]

    r1_copies = []
    for step in range(1, planes):
        make_bias(p_peers[step])
        for step_z in range(layers):
            for copy in p_copies[step, step_z]:
                copy.wait_recv()
        compute(p_peers[step], False)
        if step == planes - 1:
            back = remote(dq_acc.at[1], dq_in, pair_send.at[4], pair_recv.at[4], partner)
            back.start()
            pair_copies.append(back)
        out1[step - 1, 0] = dk_acc[...].astype(jnp.bfloat16)
        out1[step - 1, 1] = dv_acc[...].astype(jnp.bfloat16)
        copy = remote(
            out1.at[step - 1], in1.at[step - 1], r1_send.at[step - 1], r1_recv.at[step - 1], beside(step)
        )
        copy.start()
        r1_copies.append(copy)

    for copy in r1_copies:
        copy.wait_recv()
    r2_copies = []

    def layer_sum(layer):
        place = key_rows_of(layer)
        total = own[:, place]
        for step in range(1, planes):
            total = total + in1[step - 1, :, place].astype(jnp.float32)
        return total

    for step in range(1, layers):
        out2[step - 1] = layer_sum(z_peers[step]).astype(jnp.bfloat16)
        copy = remote(
            out2.at[step - 1], in2.at[step - 1], r2_send.at[step - 1], r2_recv.at[step - 1], above(step)
        )
        copy.start()
        r2_copies.append(copy)
    total = layer_sum(z)

    pair_copies[4].wait_recv()
    for h in range(heads):
        part = slice(h * width, (h + 1) * width)
        dq_ref[:, part] = ((dq_acc[0, h] + dq_in[h]) * inv_root).T

    for copy in r2_copies:
        copy.wait_recv()
    for step in range(1, layers):
        total = total + in2[step - 1].astype(jnp.float32)
    dk_ref[...] = total[0] * inv_root
    dv_ref[...] = total[1]

    sent = pair_copies + r1_copies + r2_copies
    for pair in list(z_copies.values()) + list(p_copies.values()):
        sent += pair
    for copy in sent:
        copy.wait_send()


def solution(mesh):
    planes, layers = mesh.shape["pb"] // 2, mesh.shape["kv"]

    def step(queries, key_rows, value_rows, output, out_grad, log_norm, positions):
        rows, columns = queries.shape
        keys, width = key_rows.shape
        heads = log_norm.shape[0]
        column = layers * keys
        low, full = jnp.bfloat16, jnp.float32
        vmem = pl.BlockSpec(memory_space=pltpu.VMEM)
        dma = pltpu.SemaphoreType.DMA
        return pl.pallas_call(
            functools.partial(kernel, planes, layers),
            out_shape=(
                jax.ShapeDtypeStruct((rows, columns), full),
                jax.ShapeDtypeStruct((keys, width), full),
                jax.ShapeDtypeStruct((keys, width), full),
            ),
            in_specs=[vmem] * 7,
            out_specs=(vmem, vmem, vmem),
            scratch_shapes=[
                pltpu.VMEM((2 * rows, columns), low),
                pltpu.VMEM((2 * rows, columns), low),
                pltpu.VMEM((planes, column, width), low),
                pltpu.VMEM((planes, column, width), low),
                pltpu.VMEM((heads, 2 * rows), full),
                pltpu.VMEM((heads, 2 * rows), full),
                pltpu.VMEM((column, 2 * rows), full),
                pltpu.VMEM((column, width), full),
                pltpu.VMEM((column, width), full),
                pltpu.VMEM((2, heads, width, rows), full),
                pltpu.VMEM((heads, width, rows), full),
                pltpu.VMEM((2, column, width), full),
                pltpu.VMEM((planes - 1, 2, column, width), low),
                pltpu.VMEM((planes - 1, 2, column, width), low),
                pltpu.VMEM((layers - 1, 2, keys, width), low),
                pltpu.VMEM((layers - 1, 2, keys, width), low),
                dma((5,)), dma((5,)),
                dma((layers - 1, 2)), dma((layers - 1, 2)),
                dma((planes - 1, layers, 2)), dma((planes - 1, layers, 2)),
                dma((planes - 1,)), dma((planes - 1,)),
                dma((layers - 1,)), dma((layers - 1,)),
            ],
            compiler_params=pltpu.CompilerParams(
                collective_id=0, has_side_effects=True, vmem_limit_bytes=60 * 2**20
            ),
        )(queries, key_rows, value_rows, output, out_grad, log_norm, positions.reshape(-1, rows))

    return jax.shard_map(
        step,
        mesh=mesh,
        in_specs=(
            P(("pb", "kv"), None),
            P(("kv", "pb"), None),
            P(("kv", "pb"), None),
            P(("pb", "kv"), None),
            P(("pb", "kv"), None),
            P(None, ("pb", "kv")),
            P(),
        ),
        out_specs=(P(("pb", "kv"), None), P(("kv", "pb"), None), P(("kv", "pb"), None)),
        check_vma=False,
    )
```
